512 devices in a mesh: row: 16 (over z), col: 16 (over x, y), layer: 2 (over core).
Axes of the slice: x: 4, y: 4, z: 16, core: 2. Of those that a mesh axis runs over, the one named last changes fastest.
Arguments:
- a_tiles: bfloat16 [16, 16, 2, 512, 512], P('row', 'col'), as said below
- a_where: int32 [16, 16, 2], P('row', 'col'), may hold values from 0 to 3, as said below
- a_count: int32 [16, 16], P('row', 'col'), may hold values from 1 to 2, as said below
- b_slab: bfloat16 [16, 16, 1024, 384], P('row', 'col'), may hold values from -6 to 6
Outputs:
- flow_next: float32 [16384, 6144], P(('row', 'layer'), 'col')
The draws below stay inside these ranges and needn't reach their ends.
Inputs may be any that keep to these rules, and one draw needn't show every extreme that they name: `a_where`: the positions of the slots of one block are distinct. The live slots of a block are its first a_count ones; some block has all 2 slots live. `a_tiles`: entries of slots that are not live are ignored.
All inputs are finite; a program needn't handle non-finite values.
Results may differ from the reference program's by a relative error of at most 0.0003.
Values may be sent and summed in bfloat16 or wider, within the bound.
No kernel may reach another device: no remote copies, remote signals or barrier semaphores. Data moves between devices by JAX's collectives and lax.ppermute only.
A program may use at most 64 MiB of HBM per device.

```python
import math
import jax
import jax.numpy as jnp
from jax import lax

TILE = 512
SPAN = 2
SLOTS = 2
COLS = 384
GRID = 16


def draw_a_tiles(key, part):
    key_one = jax.random.fold_in(jax.random.fold_in(key, 11), 0)
    tile_shape = (GRID, GRID, SLOTS, TILE, TILE)
    rising = jnp.arange(GRID, dtype=jnp.float32) / max(GRID - 1, 1)
    entries = jax.random.normal(key_one, tile_shape, jnp.float32)
    amplitude = (3.0 ** (0.5 * rising))[:, None, None, None, None]
    return (entries * amplitude / math.sqrt(TILE * GRID)).astype(jnp.bfloat16)


def draw_a_where(key, part):
    scores = jax.random.randint(jax.random.fold_in(key, 23), (GRID, GRID, SPAN * SPAN), 0, 1 << 20)
    scores = scores * (SPAN * SPAN) + jnp.arange(SPAN * SPAN, dtype=jnp.int32)
    ordering = jnp.argsort(scores, axis=-1)
    return ordering[:, :, :SLOTS].astype(jnp.int32)


def draw_a_count(key, part):
    key_one, key_two = jax.random.split(jax.random.fold_in(key, 37))
    counts = jax.random.randint(key_one, (GRID, GRID), 1, SLOTS + 1)
    chosen = jax.random.randint(key_two, (), 0, GRID * GRID)
    flat_ids = jnp.arange(GRID * GRID, dtype=jnp.int32).reshape(GRID, GRID)
    return jnp.where(flat_ids == chosen, SLOTS, counts).astype(jnp.int32)


def block_scale(stream_key, dims, cuts, low, top_value):
    def one(axis_at, shards_of):
        steps = jax.random.uniform(jax.random.fold_in(jax.random.fold_in(stream_key, 6), axis_at), (shards_of,), jnp.float32, low / len(cuts), top_value / len(cuts))
        return jnp.repeat(jnp.exp(steps), dims[axis_at] // shards_of).reshape((-1,) + (1,) * (len(dims) - axis_at - 1))

    factor_of = one(*cuts[0])
    for cut in cuts[1:]:
        factor_of = factor_of * one(*cut)
    return factor_of


def centred(stream_key, extent, spread, limit, cuts=(), kind=jnp.bfloat16):
    factor_of = block_scale(stream_key, extent, cuts, -0.22, 0.18) if cuts else 1.0
    values = jax.random.normal(stream_key, extent, jnp.float32) * spread * factor_of
    return jnp.minimum(jnp.maximum(values, -limit), limit).astype(kind)


def setup_inputs(seed: int = 0) -> dict:
    keys = jax.random.split(jax.random.key(seed), 5)
    a_tiles = draw_a_tiles(jax.random.fold_in(keys[4], 71), 0)
    a_where = draw_a_where(jax.random.fold_in(keys[4], 71), 0)
    a_count = draw_a_count(jax.random.fold_in(keys[4], 71), 0)
    b_slab = centred(keys[3], (GRID, GRID, SPAN * TILE, COLS), 1.0, 6.0, ((0, 16), (1, 16)))
    return {"a_tiles": a_tiles, "a_where": a_where, "a_count": a_count, "b_slab": b_slab}


def roll_column(column_blocks, shift_by):
    return jnp.roll(column_blocks, shift_by, axis=0)


def reference(a_tiles, a_where, a_count, b_slab):
    grid_size = a_tiles.shape[0]
    tile_size = a_tiles.shape[-1]
    slab_cols = b_slab.shape[-1]
    matrix_order = grid_size * SPAN * tile_size
    block_ids = jnp.arange(grid_size, dtype=jnp.int32)
    aligned = jax.vmap(roll_column, in_axes=(1, 0), out_axes=1)(b_slab, block_ids)
    slab_full = aligned.transpose(0, 2, 1, 3).reshape(matrix_order, grid_size * slab_cols).astype(jnp.float32)
    positions = jnp.arange(SPAN * SPAN, dtype=jnp.int32)
    slot_ids = jnp.arange(SLOTS, dtype=jnp.int32)

    def band_rows(block_row):
        tile_data = a_tiles[block_row].astype(jnp.float32)
        live_mask = (slot_ids[None, :] < a_count[block_row][:, None]).astype(jnp.float32)
        placement = (a_where[block_row][:, :, None] == positions[None, None, :]).astype(jnp.float32)
        placement = placement * live_mask[:, :, None]
        dense_blocks = jnp.einsum("jsp,jsab->jpab", placement, tile_data, precision=lax.Precision.HIGHEST)
        dense_blocks = jnp.roll(dense_blocks, block_row, axis=0)
        dense_blocks = dense_blocks.reshape(grid_size, SPAN, SPAN, tile_size, tile_size)
        dense_blocks = dense_blocks.transpose(1, 3, 0, 2, 4).reshape(SPAN * tile_size, matrix_order)
        return jnp.dot(dense_blocks, slab_full, precision=lax.Precision.HIGHEST)

    product = lax.map(band_rows, block_ids).reshape(matrix_order, grid_size * slab_cols)
    inflated = product * product
    column_mass = jnp.sum(inflated, axis=0) / matrix_order
    return inflated / (column_mass + 1e-6)
```

```python
import jax
import jax.numpy as jnp
from jax import lax
from jax.experimental import pallas as pl
from jax.experimental.pallas import tpu as pltpu
from jax.sharding import PartitionSpec as P


SPAN = 2
SIDE = 4
PAD = 16
DEAD = SPAN * SPAN


def torus_pairs(step, layers):
    pairs = []
    for x in range(SIDE):
        for y in range(SIDE):
            for core in range(layers):
                sign = 1 - 2 * core
                to_x, to_y = (x + sign * step[0]) % SIDE, (y + sign * step[1]) % SIDE
                pairs.append(((x * SIDE + y) * layers + core, (to_x * SIDE + to_y) * layers + core))
    return pairs


def shift(value, step, sign, layers):
    return lax.ppermute(value, ("col", "layer"), torus_pairs((sign * step[0], sign * step[1]), layers))


def gather_line(value, step, layers):
    before = shift(value, step, 1, layers)
    after = shift(value, step, -1, layers)
    return [value, before, after, shift(before, step, 1, layers)]


def product_kernel(table, *refs):
    tile_refs = refs[:8]
    slab, keep, send, mass, buffers, sums, arrived = refs[8:]
    rows, depth = keep.shape[0], buffers.shape[1]
    stride = rows + PAD

    def fetch(item):
        block = table[1, item] * SPAN + table[0, item] % SPAN
        start = pl.multiple_of(block * depth, depth)
        return pltpu.make_async_copy(slab.at[pl.ds(start, depth), :], buffers.at[item], arrived.at[item])

    def start_one(item, carry):
        @pl.when(table[0, item] < DEAD)
        def _():
            fetch(item).start()

        return carry

    lax.fori_loop(0, 32, start_one, 0)
    sums[...] = jnp.zeros_like(sums)
    for group, tiles in enumerate(tile_refs):

        def multiply(inner, carry, group=group, tiles=tiles):
            item = group * 4 + inner

            @pl.when(table[0, item] < DEAD)
            def _():
                fetch(item).wait()
                piece = tiles[pl.ds(pl.multiple_of(inner * stride, PAD), rows), :]
                sums[table[0, item] // SPAN] += jnp.dot(
                    piece, buffers[item], preferred_element_type=jnp.float32
                )

            return carry

        lax.fori_loop(0, 4, multiply, 0)
    mine = table[2, 0]
    kept = sums[mine]
    given = sums[1 - mine]
    kept = kept * kept
    given = given * given
    keep[...] = kept
    send[...] = given
    mass[...] = jnp.sum(kept, axis=0, keepdims=True) + jnp.sum(given, axis=0, keepdims=True)


def local(a_tiles, a_where, a_count, b_slab):
    layers = lax.axis_size("layer")
    grid_size = lax.axis_size("col")
    row = lax.axis_index("row")
    col = lax.axis_index("col")
    layer = lax.axis_index("layer")
    slots, tile_size = a_tiles.shape[2], a_tiles.shape[-1]
    slab_cols = b_slab.shape[-1]
    rows = tile_size // layers

    slab_half = lax.dynamic_slice(b_slab[0, 0], (layer * tile_size, 0), (tile_size, slab_cols))
    slab = lax.all_gather(slab_half, ("row", "layer"), axis=0, tiled=True)

    live = jnp.arange(slots, dtype=jnp.int32) < a_count[0, 0]
    codes = jnp.where(live, a_where[0, 0], DEAD).astype(jnp.bfloat16)
    lines = []
    steps = (((0, 1), (1, 0)), ((1, 0), (0, 1)))
    for slot, (first, second) in enumerate(steps):
        piece = lax.dynamic_slice(a_tiles[0, 0], (slot, layer * rows, 0), (1, rows, tile_size))[0]
        code = jnp.broadcast_to(codes[slot], (PAD, tile_size))
        lines.append(gather_line(jnp.concatenate([piece, code], 0), first, layers))
    tiles = []
    for (first, second), line in zip(steps, lines):
        tiles += gather_line(jnp.concatenate(line, 0), second, layers)

    sign = 1 - 2 * layer
    offset = jnp.array([0, -1, 1, -2], jnp.int32) * sign
    here_x, here_y = col // SIDE, col % SIDE
    far_x, far_y = (here_x + offset) % SIDE, (here_y + offset) % SIDE
    source = jnp.stack([far_x[:, None] * SIDE + far_y[None, :], far_x[None, :] * SIDE + far_y[:, None]])
    slab_row = (row + source - col) % grid_size
    stride = rows + PAD
    found = jnp.concatenate([t.reshape(4, stride, tile_size)[:, rows, 0] for t in tiles])
    table = jnp.stack(
        [found.astype(jnp.int32), slab_row.reshape(-1), jnp.broadcast_to(layer, (32,))]
    )

    vmem = pl.BlockSpec(memory_space=pltpu.VMEM)
    flops = 2 * 32 * rows * tile_size * slab_cols
    keep, send, mass = pl.pallas_call(
        product_kernel,
        out_shape=(
            jax.ShapeDtypeStruct((rows, slab_cols), jnp.float32),
            jax.ShapeDtypeStruct((rows, slab_cols), jnp.float32),
            jax.ShapeDtypeStruct((1, slab_cols), jnp.float32),
        ),
        in_specs=[pl.BlockSpec(memory_space=pltpu.SMEM)]
        + [vmem] * 8
        + [pl.BlockSpec(memory_space=pl.ANY)],
        out_specs=(vmem, vmem, vmem),
        scratch_shapes=[
            pltpu.VMEM((32, tile_size, slab_cols), jnp.bfloat16),
            pltpu.VMEM((SPAN, rows, slab_cols), jnp.float32),
            pltpu.SemaphoreType.DMA((32,)),
        ],
        compiler_params=pltpu.CompilerParams(vmem_limit_bytes=40 << 20),
        cost_estimate=pl.CostEstimate(flops=flops, bytes_accessed=20 << 20, transcendentals=0),
    )(table, *tiles, slab)

    other = lax.ppermute(send, "layer", [(0, 1), (1, 0)])
    members = lax.axis_size("row") * layers
    spread = lax.all_to_all(
        jnp.broadcast_to(mass, (members, slab_cols)), ("row", "layer"), 0, 0, tiled=True
    )
    matrix_order = grid_size * SPAN * tile_size
    column_mass = jnp.sum(spread, axis=0) / matrix_order
    upper = layer == 0
    inflated = jnp.concatenate([jnp.where(upper, keep, other), jnp.where(upper, other, keep)], 0)
    return inflated / (column_mass + 1e-06)


def solution(mesh):
    in_specs = (
        P("row", "col", None, None, None),
        P("row", "col", None),
        P("row", "col"),
        P("row", "col", None, None),
    )
    out_specs = P(("row", "layer"), "col")
    return jax.shard_map(local, mesh=mesh, in_specs=in_specs, out_specs=out_specs, check_vma=False)
```

```python
import jax
import jax.numpy as jnp
from jax import lax
from jax.experimental import pallas as pl
from jax.experimental.pallas import tpu as pltpu
from jax.sharding import PartitionSpec as P


SPAN = 2
SIDE = 4
PAD = 16
DEAD = SPAN * SPAN


def torus_pairs(step, layers):
    pairs = []
    for x in range(SIDE):
        for y in range(SIDE):
            for core in range(layers):
                sign = 1 - 2 * core
                to_x, to_y = (x + sign * step[0]) % SIDE, (y + sign * step[1]) % SIDE
                pairs.append(((x * SIDE + y) * layers + core, (to_x * SIDE + to_y) * layers + core))
    return pairs


def shift(value, step, sign, layers):
    return lax.ppermute(value, ("col", "layer"), torus_pairs((sign * step[0], sign * step[1]), layers))


def gather_line(value, step, layers):
    before = shift(value, step, 1, layers)
    after = shift(value, step, -1, layers)
    return [value, before, after, shift(before, step, 1, layers)]


def product_kernel(table, *refs):
    tile_refs = refs[:8]
    slab, keep, send, mass, pieces, blocks, sums, order, target, piece_sem, block_sem, sent = refs[8:]
    rows, depth = keep.shape[0], blocks.shape[1]
    stride = rows + PAD

    def fetches(item, tiles, inner):
        block = table[1, item] * SPAN + table[0, item] % SPAN
        start = pl.multiple_of(block * depth, depth)
        first = pl.multiple_of(inner * stride, PAD)
        return (
            pltpu.make_async_copy(tiles.at[pl.ds(first, rows), :], pieces.at[item], piece_sem.at[item]),
            pltpu.make_async_copy(slab.at[pl.ds(start, depth), :], blocks.at[item], block_sem.at[item]),
        )

    def enlist(count, item, tiles, inner):
        for copy in fetches(item, tiles, inner):
            copy.start()
        order[count] = item
        target[count] = table[0, item] // SPAN

    for item in range(16):
        enlist(item, item, tile_refs[item // 4], item % 4)
    count = jnp.int32(16)
    for group in range(4, 8):

        def enlist_live(inner, count, group=group):
            item = group * 4 + inner
            live = table[0, item] < DEAD

            @pl.when(live)
            def _():
                enlist(count, item, tile_refs[group], inner)

            return count + live.astype(jnp.int32)

        count = lax.fori_loop(0, 4, enlist_live, count)
    for spare in range(3):
        order[count + spare] = 0
        target[count + spare] = SPAN
    sums[...] = jnp.zeros_like(sums)

    def batch(step, carry):
        for lane in range(4):
            place = step * 4 + lane

            @pl.when(place < count)
            def _():
                for copy in fetches(order[place], tile_refs[0], 0):
                    copy.wait()

        for lane in range(4):
            item = order[step * 4 + lane]
            sums[target[step * 4 + lane]] += jnp.dot(
                pieces[item], blocks[item], preferred_element_type=jnp.float32
            )
        return carry

    lax.fori_loop(0, (count + 3) // 4, batch, 0)
    mine = table[2, 0]
    given = sums[1 - mine]
    given = given * given
    sums[1 - mine] = given
    copy = pltpu.make_async_copy(sums.at[1 - mine], send, sent)
    copy.start()
    kept = sums[mine]
    kept = kept * kept
    keep[...] = kept
    total = jnp.sum(kept, axis=0, keepdims=True) + jnp.sum(given, axis=0, keepdims=True)
    mass[...] = jnp.broadcast_to(total[None], mass.shape)
    copy.wait()


def local(a_tiles, a_where, a_count, b_slab):
    layers = lax.axis_size("layer")
    grid_size = lax.axis_size("col")
    row = lax.axis_index("row")
    col = lax.axis_index("col")
    layer = lax.axis_index("layer")
    slots, tile_size = a_tiles.shape[2], a_tiles.shape[-1]
    slab_cols = b_slab.shape[-1]
    rows = tile_size // layers

    slab_half = lax.dynamic_slice(b_slab[0, 0], (layer * tile_size, 0), (tile_size, slab_cols))
    slab = lax.all_gather(slab_half, ("row", "layer"), axis=0, tiled=True)

    live = jnp.arange(slots, dtype=jnp.int32) < a_count[0, 0]
    codes = jnp.where(live, a_where[0, 0], DEAD).astype(jnp.bfloat16)
    lines = []
    steps = (((0, 1), (1, 0)), ((1, 0), (0, 1)))
    for slot, (first, second) in enumerate(steps):
        piece = lax.dynamic_slice(a_tiles[0, 0], (slot, layer * rows, 0), (1, rows, tile_size))[0]
        code = jnp.broadcast_to(codes[slot], (PAD, tile_size))
        lines.append(gather_line(jnp.concatenate([piece, code], 0), first, layers))
    tiles = []
    for (first, second), line in zip(steps, lines):
        tiles += gather_line(jnp.concatenate(line, 0), second, layers)

    sign = 1 - 2 * layer
    offset = jnp.array([0, -1, 1, -2], jnp.int32) * sign
    here_x, here_y = col // SIDE, col % SIDE
    far_x, far_y = (here_x + offset) % SIDE, (here_y + offset) % SIDE
    source = jnp.stack([far_x[:, None] * SIDE + far_y[None, :], far_x[None, :] * SIDE + far_y[:, None]])
    slab_row = (row + source - col) % grid_size
    stride = rows + PAD
    found = jnp.concatenate([t.reshape(4, stride, tile_size)[:, rows, 0] for t in tiles])
    table = jnp.stack(
        [found.astype(jnp.int32), slab_row.reshape(-1), jnp.broadcast_to(layer, (32,))]
    )

    vmem = pl.BlockSpec(memory_space=pltpu.VMEM)
    hbm = pl.BlockSpec(memory_space=pl.ANY)
    members = lax.axis_size("row") * layers
    flops = 2 * 32 * rows * tile_size * slab_cols
    keep, send, mass = pl.pallas_call(
        product_kernel,
        out_shape=(
            jax.ShapeDtypeStruct((rows, slab_cols), jnp.float32),
            jax.ShapeDtypeStruct((rows, slab_cols), jnp.float32),
            jax.ShapeDtypeStruct((members, 1, slab_cols), jnp.float32),
        ),
        in_specs=[pl.BlockSpec(memory_space=pltpu.SMEM)] + [hbm] * 9,
        out_specs=(vmem, hbm, vmem),
        scratch_shapes=[
            pltpu.VMEM((32, rows, tile_size), jnp.bfloat16),
            pltpu.VMEM((32, tile_size, slab_cols), jnp.bfloat16),
            pltpu.VMEM((SPAN + 1, rows, slab_cols), jnp.float32),
            pltpu.SMEM((36,), jnp.int32),
            pltpu.SMEM((36,), jnp.int32),
            pltpu.SemaphoreType.DMA((32,)),
            pltpu.SemaphoreType.DMA((32,)),
            pltpu.SemaphoreType.DMA,
        ],
        compiler_params=pltpu.CompilerParams(vmem_limit_bytes=60 << 20),
        cost_estimate=pl.CostEstimate(flops=flops, bytes_accessed=20 << 20, transcendentals=0),
    )(table, *tiles, slab)

    other = lax.ppermute(send, "layer", [(0, 1), (1, 0)])
    spread = lax.all_to_all(mass, ("row", "layer"), 0, 0, tiled=True)
    matrix_order = grid_size * SPAN * tile_size
    column_mass = jnp.sum(spread, axis=(0, 1)) / matrix_order
    upper = layer == 0
    inflated = jnp.concatenate([jnp.where(upper, keep, other), jnp.where(upper, other, keep)], 0)
    return inflated / (column_mass + 1e-06)


def solution(mesh):
    in_specs = (
        P("row", "col", None, None, None),
        P("row", "col", None),
        P("row", "col"),
        P("row", "col", None, None),
    )
    out_specs = P(("row", "layer"), "col")
    return jax.shard_map(local, mesh=mesh, in_specs=in_specs, out_specs=out_specs, check_vma=False)
```

```python
import jax
import jax.numpy as jnp
from jax import lax
from jax.experimental import pallas as pl
from jax.experimental.pallas import tpu as pltpu
from jax.sharding import PartitionSpec as P


SPAN = 2
SIDE = 4
PAD = 16
DEAD = SPAN * SPAN


def torus_pairs(step, layers):
    pairs = []
    for x in range(SIDE):
        for y in range(SIDE):
            for core in range(layers):
                sign = 1 - 2 * core
                to_x, to_y = (x + sign * step[0]) % SIDE, (y + sign * step[1]) % SIDE
                pairs.append(((x * SIDE + y) * layers + core, (to_x * SIDE + to_y) * layers + core))
    return pairs


def shift(value, step, sign, layers):
    return lax.ppermute(value, ("col", "layer"), torus_pairs((sign * step[0], sign * step[1]), layers))


def gather_line(value, step, layers):
    before = shift(value, step, 1, layers)
    after = shift(value, step, -1, layers)
    return [value, before, after, shift(before, step, 1, layers)]


def product_kernel(table, *refs):
    tile_refs = refs[:8]
    slab, keep, send, mass, pieces, blocks, sums, spread, order, target = refs[8:18]
    piece_sem, block_sem, out_sem = refs[18:]
    rows, depth = pieces.shape[1], blocks.shape[1]
    stride = rows + PAD

    def fetches(item, tiles, inner):
        block = table[1, item] * SPAN + table[0, item] % SPAN
        start = pl.multiple_of(block * depth, depth)
        first = pl.multiple_of(inner * stride, PAD)
        return (
            pltpu.make_async_copy(tiles.at[pl.ds(first, rows), :], pieces.at[item], piece_sem.at[item]),
            pltpu.make_async_copy(slab.at[pl.ds(start, depth), :], blocks.at[item], block_sem.at[item]),
        )

    def start(item, tiles, inner):
        for copy in fetches(item, tiles, inner):
            copy.start()

    def wait(item):
        for copy in fetches(item, tile_refs[0], 0):
            copy.wait()

    def add_product(item, half):
        sums[half] += jnp.dot(pieces[item], blocks[item], preferred_element_type=jnp.float32)

    for item in range(16):
        start(item, tile_refs[item // 4], item % 4)
    sums[:SPAN] = jnp.zeros((SPAN,) + sums.shape[1:], jnp.float32)
    count = jnp.int32(0)
    for group in range(4):
        for item in range(group * 4, group * 4 + 4):
            wait(item)
        for item in range(group * 4, group * 4 + 4):
            add_product(item, table[0, item] // SPAN)
        for inner in range(4):
            item = 16 + group * 4 + inner
            live = table[0, item] < DEAD

            @pl.when(live)
            def _(item=item, inner=inner, group=group, count=count):
                start(item, tile_refs[4 + group], inner)
                order[count] = item
                target[count] = table[0, item] // SPAN

            count = count + live.astype(jnp.int32)
    for spare in range(3):
        order[count + spare] = 0
        target[count + spare] = SPAN

    def batch(step, carry):
        for lane in range(4):
            place = step * 4 + lane

            @pl.when(place < count)
            def _(place=place):
                wait(order[place])

        for lane in range(4):
            add_product(order[step * 4 + lane], target[step * 4 + lane])
        return carry

    lax.fori_loop(0, (count + 3) // 4, batch, 0)
    mine = table[2, 0]
    outs = []
    total = jnp.zeros((1, sums.shape[2]), jnp.float32)
    for at, (half, out) in enumerate(((1 - mine, send), (mine, keep))):
        value = sums[half]
        value = value * value
        sums[half] = value
        outs.append(pltpu.make_async_copy(sums.at[half], out, out_sem.at[at]))
        outs[-1].start()
        total = total + jnp.sum(value, axis=0, keepdims=True)
    spread[...] = jnp.broadcast_to(total[None], spread.shape)
    outs.append(pltpu.make_async_copy(spread, mass, out_sem.at[2]))
    outs[-1].start()
    for copy in outs:
        copy.wait()


def local(a_tiles, a_where, a_count, b_slab):
    layers = lax.axis_size("layer")
    grid_size = lax.axis_size("col")
    row = lax.axis_index("row")
    col = lax.axis_index("col")
    layer = lax.axis_index("layer")
    slots, tile_size = a_tiles.shape[2], a_tiles.shape[-1]
    slab_cols = b_slab.shape[-1]
    rows = tile_size // layers

    slab_half = lax.dynamic_slice(b_slab[0, 0], (layer * tile_size, 0), (tile_size, slab_cols))
    slab = lax.all_gather(slab_half, ("row", "layer"), axis=0, tiled=True)

    live = jnp.arange(slots, dtype=jnp.int32) < a_count[0, 0]
    codes = jnp.where(live, a_where[0, 0], DEAD).astype(jnp.bfloat16)
    lines = []
    steps = (((0, 1), (1, 0)), ((1, 0), (0, 1)))
    for slot, (first, second) in enumerate(steps):
        piece = lax.dynamic_slice(a_tiles[0, 0], (slot, layer * rows, 0), (1, rows, tile_size))[0]
        code = jnp.broadcast_to(codes[slot], (PAD, tile_size))
        lines.append(gather_line(jnp.concatenate([piece, code], 0), first, layers))
    tiles = []
    for (first, second), line in zip(steps, lines):
        tiles += gather_line(jnp.concatenate(line, 0), second, layers)

    sign = 1 - 2 * layer
    offset = jnp.array([0, -1, 1, -2], jnp.int32) * sign
    here_x, here_y = col // SIDE, col % SIDE
    far_x, far_y = (here_x + offset) % SIDE, (here_y + offset) % SIDE
    source = jnp.stack([far_x[:, None] * SIDE + far_y[None, :], far_x[None, :] * SIDE + far_y[:, None]])
    slab_row = (row + source - col) % grid_size
    stride = rows + PAD
    found = jnp.concatenate([t.reshape(4, stride, tile_size)[:, rows, 0] for t in tiles])
    table = jnp.stack(
        [found.astype(jnp.int32), slab_row.reshape(-1), jnp.broadcast_to(layer, (32,))]
    )

    hbm = pl.BlockSpec(memory_space=pl.ANY)
    members = lax.axis_size("row") * layers
    flops = 2 * 32 * rows * tile_size * slab_cols
    keep, send, mass = pl.pallas_call(
        product_kernel,
        out_shape=(
            jax.ShapeDtypeStruct((rows, slab_cols), jnp.float32),
            jax.ShapeDtypeStruct((rows, slab_cols), jnp.float32),
            jax.ShapeDtypeStruct((members, 1, slab_cols), jnp.float32),
        ),
        in_specs=[pl.BlockSpec(memory_space=pltpu.SMEM)] + [hbm] * 9,
        out_specs=(hbm, hbm, hbm),
        scratch_shapes=[
            pltpu.VMEM((32, rows, tile_size), jnp.bfloat16),
            pltpu.VMEM((32, tile_size, slab_cols), jnp.bfloat16),
            pltpu.VMEM((SPAN + 1, rows, slab_cols), jnp.float32),
            pltpu.VMEM((members, 1, slab_cols), jnp.float32),
            pltpu.SMEM((20,), jnp.int32),
            pltpu.SMEM((20,), jnp.int32),
            pltpu.SemaphoreType.DMA((32,)),
            pltpu.SemaphoreType.DMA((32,)),
            pltpu.SemaphoreType.DMA((3,)),
        ],
        compiler_params=pltpu.CompilerParams(vmem_limit_bytes=60 << 20),
        cost_estimate=pl.CostEstimate(flops=flops, bytes_accessed=20 << 20, transcendentals=0),
    )(table, *tiles, slab)

    matrix_order = grid_size * SPAN * tile_size
    parts = lax.all_to_all(mass, ("row", "layer"), 0, 0, tiled=True)
    other = lax.ppermute(send, "layer", [(0, 1), (1, 0)])
    lower = layer == 0
    halves = jnp.where(lower, keep, other), jnp.where(lower, other, keep)
    column_mass = jnp.sum(parts, axis=(0, 1)) / matrix_order
    return jnp.concatenate(halves, 0) / (column_mass + 1e-06)


def solution(mesh):
    in_specs = (
        P("row", "col", None, None, None),
        P("row", "col", None),
        P("row", "col"),
        P("row", "col", None, None),
    )
    out_specs = P(("row", "layer"), "col")
    return jax.shard_map(local, mesh=mesh, in_specs=in_specs, out_specs=out_specs, check_vma=False)
```

```python
import jax
import jax.numpy as jnp
from jax import lax
from jax.experimental import pallas as pl
from jax.experimental.pallas import tpu as pltpu
from jax.sharding import PartitionSpec as P


SPAN = 2
SIDE = 4
PAD = 16
DEAD = SPAN * SPAN


def torus_pairs(step, layers):
    pairs = []
    for x in range(SIDE):
        for y in range(SIDE):
            for core in range(layers):
                sign = 1 - 2 * core
                to_x, to_y = (x + sign * step[0]) % SIDE, (y + sign * step[1]) % SIDE
                pairs.append(((x * SIDE + y) * layers + core, (to_x * SIDE + to_y) * layers + core))
    return pairs


def shift(value, step, sign, layers):
    return lax.ppermute(value, ("col", "layer"), torus_pairs((sign * step[0], sign * step[1]), layers))


def gather_line(value, step, layers):
    before = shift(value, step, 1, layers)
    after = shift(value, step, -1, layers)
    return [value, before, after, shift(before, step, 1, layers)]


def product_kernel(table, *refs):
    tile_refs = refs[:8]
    slab, keep, send, mass, pieces, blocks, sums, spread, order, target, source = refs[8:19]
    piece_sem, block_sem, out_sem = refs[19:]
    rows, depth = pieces.shape[1], blocks.shape[1]
    stride = rows + PAD

    def fetch_piece(item, tiles, inner):
        first = pl.multiple_of(inner * stride, PAD)
        return pltpu.make_async_copy(tiles.at[pl.ds(first, rows), :], pieces.at[item], piece_sem.at[item])

    def fetch_block(item):
        block = table[1, item] * SPAN + table[0, item] % SPAN
        first = pl.multiple_of(block * depth, depth)
        return pltpu.make_async_copy(slab.at[pl.ds(first, depth), :], blocks.at[item], block_sem.at[item])

    def add_product(item, block, half):
        sums[half] += jnp.dot(pieces[item], blocks[block], preferred_element_type=jnp.float32)

    for item in range(16):
        fetch_piece(item, tile_refs[item // 4], item % 4).start()
        fetch_block(item).start()
    sums[:SPAN] = jnp.zeros((SPAN,) + sums.shape[1:], jnp.float32)
    count = jnp.int32(0)
    for group in range(4):
        for item in range(group * 4, group * 4 + 4):
            fetch_piece(item, tile_refs[0], 0).wait()
            fetch_block(item).wait()
        for item in range(group * 4, group * 4 + 4):
            add_product(item, item, table[0, item] // SPAN)
        for inner in range(4):
            item, mate = 16 + group * 4 + inner, inner * 4 + group
            live = table[0, item] < DEAD
            own = table[0, item] % SPAN != table[0, mate] % SPAN

            @pl.when(live)
            def _(item=item, inner=inner, group=group, count=count, own=own, mate=mate):
                fetch_piece(item, tile_refs[4 + group], inner).start()
                pl.when(own)(lambda: fetch_block(item).start())
                order[count] = item
                source[count] = jnp.where(own, item, mate)
                target[count] = table[0, item] // SPAN

            count = count + live.astype(jnp.int32)
    for spare in range(3):
        order[count + spare] = 0
        source[count + spare] = 0
        target[count + spare] = SPAN

    def batch(step, carry):
        for lane in range(4):
            place = step * 4 + lane

            @pl.when(place < count)
            def _(place=place):
                item = order[place]
                fetch_piece(item, tile_refs[0], 0).wait()
                pl.when(source[place] == item)(lambda: fetch_block(item).wait())

        for lane in range(4):
            place = step * 4 + lane
            add_product(order[place], source[place], target[place])
        return carry

    lax.fori_loop(0, (count + 3) // 4, batch, 0)
    mine = table[2, 0]
    outs = []
    total = jnp.zeros((1, sums.shape[2]), jnp.float32)
    for at, (half, out) in enumerate(((1 - mine, send), (mine, keep))):
        value = sums[half]
        value = value * value
        sums[half] = value
        outs.append(pltpu.make_async_copy(sums.at[half], out, out_sem.at[at]))
        outs[-1].start()
        total = total + jnp.sum(value, axis=0, keepdims=True)
    spread[...] = jnp.broadcast_to(total[None], spread.shape)
    outs.append(pltpu.make_async_copy(spread, mass, out_sem.at[2]))
    outs[-1].start()
    for copy in outs:
        copy.wait()


def local(a_tiles, a_where, a_count, b_slab):
    layers = lax.axis_size("layer")
    grid_size = lax.axis_size("col")
    row = lax.axis_index("row")
    col = lax.axis_index("col")
    layer = lax.axis_index("layer")
    slots, tile_size = a_tiles.shape[2], a_tiles.shape[-1]
    slab_cols = b_slab.shape[-1]
    rows = tile_size // layers

    slab_half = lax.dynamic_slice(b_slab[0, 0], (layer * tile_size, 0), (tile_size, slab_cols))
    slab = lax.all_gather(slab_half, ("row", "layer"), axis=0, tiled=True)

    live = jnp.arange(slots, dtype=jnp.int32) < a_count[0, 0]
    codes = jnp.where(live, a_where[0, 0], DEAD).astype(jnp.bfloat16)
    lines = []
    steps = (((0, 1), (1, 0)), ((1, 0), (0, 1)))
    for slot, (first, second) in enumerate(steps):
        piece = lax.dynamic_slice(a_tiles[0, 0], (slot, layer * rows, 0), (1, rows, tile_size))[0]
        code = jnp.broadcast_to(codes[slot], (PAD, tile_size))
        lines.append(gather_line(jnp.concatenate([piece, code], 0), first, layers))
    tiles = []
    for (first, second), line in zip(steps, lines):
        tiles += gather_line(jnp.concatenate(line, 0), second, layers)

    sign = 1 - 2 * layer
    offset = jnp.array([0, -1, 1, -2], jnp.int32) * sign
    here_x, here_y = col // SIDE, col % SIDE
    far_x, far_y = (here_x + offset) % SIDE, (here_y + offset) % SIDE
    source = jnp.stack([far_x[:, None] * SIDE + far_y[None, :], far_x[None, :] * SIDE + far_y[:, None]])
    slab_row = (row + source - col) % grid_size
    stride = rows + PAD
    found = jnp.concatenate([t.reshape(4, stride, tile_size)[:, rows, 0] for t in tiles])
    table = jnp.stack(
        [found.astype(jnp.int32), slab_row.reshape(-1), jnp.broadcast_to(layer, (32,))]
    )

    hbm = pl.BlockSpec(memory_space=pl.ANY)
    members = lax.axis_size("row") * layers
    flops = 2 * 32 * rows * tile_size * slab_cols
    keep, send, mass = pl.pallas_call(
        product_kernel,
        out_shape=(
            pltpu.HBM((rows, slab_cols), jnp.float32),
            pltpu.HBM((rows, slab_cols), jnp.float32),
            pltpu.HBM((members, 1, slab_cols), jnp.float32),
        ),
        in_specs=[pl.BlockSpec(memory_space=pltpu.SMEM)] + [hbm] * 9,
        out_specs=(hbm, hbm, hbm),
        scratch_shapes=[
            pltpu.VMEM((32, rows, tile_size), jnp.bfloat16),
            pltpu.VMEM((32, tile_size, slab_cols), jnp.bfloat16),
            pltpu.VMEM((SPAN + 1, rows, slab_cols), jnp.float32),
            pltpu.VMEM((members, 1, slab_cols), jnp.float32),
            pltpu.SMEM((20,), jnp.int32),
            pltpu.SMEM((20,), jnp.int32),
            pltpu.SMEM((20,), jnp.int32),
            pltpu.SemaphoreType.DMA((32,)),
            pltpu.SemaphoreType.DMA((32,)),
            pltpu.SemaphoreType.DMA((3,)),
        ],
        compiler_params=pltpu.CompilerParams(vmem_limit_bytes=44 << 20),
        cost_estimate=pl.CostEstimate(flops=flops, bytes_accessed=20 << 20, transcendentals=0),
    )(table, *tiles, slab)

    matrix_order = grid_size * SPAN * tile_size
    parts = lax.all_to_all(mass, ("row", "layer"), 0, 0, tiled=True)
    other = lax.ppermute(send, "layer", [(0, 1), (1, 0)])
    lower = layer == 0
    halves = jnp.where(lower, keep, other), jnp.where(lower, other, keep)
    column_mass = jnp.sum(parts, axis=(0, 1)) / matrix_order
    return jnp.concatenate(halves, 0) / (column_mass + 1e-06)


def solution(mesh):
    in_specs = (
        P("row", "col", None, None, None),
        P("row", "col", None),
        P("row", "col"),
        P("row", "col", None, None),
    )
    out_specs = P(("row", "layer"), "col")
    return jax.shard_map(local, mesh=mesh, in_specs=in_specs, out_specs=out_specs, check_vma=False)
```

```python
import functools

import jax
import jax.numpy as jnp
from jax import lax
from jax.experimental import pallas as pl
from jax.experimental.pallas import tpu as pltpu
from jax.sharding import PartitionSpec as P


SPAN = 2
SIDE = 4
PAD = 16
DEAD = SPAN * SPAN


def torus_pairs(step, layers):
    pairs = []
    for x in range(SIDE):
        for y in range(SIDE):
            for core in range(layers):
                sign = 1 - 2 * core
                to_x, to_y = (x + sign * step[0]) % SIDE, (y + sign * step[1]) % SIDE
                pairs.append(((x * SIDE + y) * layers + core, (to_x * SIDE + to_y) * layers + core))
    return pairs


def shift(value, step, sign, layers):
    return lax.ppermute(value, ("col", "layer"), torus_pairs((sign * step[0], sign * step[1]), layers))


def gather_line(value, step, layers):
    before = shift(value, step, 1, layers)
    after = shift(value, step, -1, layers)
    return [value, before, after, shift(before, step, 1, layers)]


def product_kernel(table, *refs):
    tile_refs = refs[:8]
    slab, keep, send, mass, pieces, blocks, sums, spread, order, target, source = refs[8:19]
    piece_sem, block_sem, out_sem = refs[19:]
    rows, depth = pieces.shape[1], blocks.shape[1]
    stride = rows + PAD

    def fetch_piece(item, tiles, inner):
        first = pl.multiple_of(inner * stride, PAD)
        return pltpu.make_async_copy(tiles.at[pl.ds(first, rows), :], pieces.at[item], piece_sem.at[item])

    def fetch_block(item):
        block = table[1, item] * SPAN + table[0, item] % SPAN
        first = pl.multiple_of(block * depth, depth)
        return pltpu.make_async_copy(slab.at[pl.ds(first, depth), :], blocks.at[item], block_sem.at[item])

    def add_product(item, block, half):
        sums[half] += jnp.dot(pieces[item], blocks[block], preferred_element_type=jnp.float32)

    for item in range(16):
        fetch_piece(item, tile_refs[item // 4], item % 4).start()
        fetch_block(item).start()
    sums[:SPAN] = jnp.zeros((SPAN,) + sums.shape[1:], jnp.float32)
    count = jnp.int32(0)
    for group in range(4):
        at_once = 1 if group == 0 else 4
        for first in range(group * 4, group * 4 + 4, at_once):
            for item in range(first, first + at_once):
                fetch_piece(item, tile_refs[0], 0).wait()
                fetch_block(item).wait()
            for item in range(first, first + at_once):
                add_product(item, item, table[0, item] // SPAN)
        for inner in range(4):
            item, mate = 16 + group * 4 + inner, inner * 4 + group
            live = table[0, item] < DEAD
            own = table[0, item] % SPAN != table[0, mate] % SPAN

            @pl.when(live)
            def _(item=item, inner=inner, group=group, count=count, own=own, mate=mate):
                fetch_piece(item, tile_refs[4 + group], inner).start()
                pl.when(own)(lambda: fetch_block(item).start())
                order[count] = item
                source[count] = jnp.where(own, item, mate)
                target[count] = table[0, item] // SPAN

            count = count + live.astype(jnp.int32)
    order[count] = 0
    source[count] = 0
    target[count] = SPAN
    batches = (count + 1) // 4

    def wait(place):
        item = order[place]
        fetch_piece(item, tile_refs[0], 0).wait()
        pl.when(source[place] == item)(lambda: fetch_block(item).wait())

    def batch(step, carry):
        for lane in range(4):
            place = step * 4 + lane
            pl.when(place < count)(functools.partial(wait, place))
        for lane in range(4):
            place = step * 4 + lane
            add_product(order[place], source[place], target[place])
        return carry

    def single(place, carry):
        wait(place)
        add_product(order[place], source[place], target[place])
        return carry

    lax.fori_loop(0, batches, batch, 0)
    lax.fori_loop(batches * 4, count, single, 0)
    mine = table[2, 0]
    outs = []
    total = jnp.zeros((1, sums.shape[2]), jnp.float32)
    for at, (half, out) in enumerate(((1 - mine, send), (mine, keep))):
        value = sums[half]
        value = value * value
        sums[half] = value
        outs.append(pltpu.make_async_copy(sums.at[half], out, out_sem.at[at]))
        outs[-1].start()
        total = total + jnp.sum(value, axis=0, keepdims=True)
    spread[...] = jnp.broadcast_to(total[None], spread.shape)
    outs.append(pltpu.make_async_copy(spread, mass, out_sem.at[2]))
    outs[-1].start()
    for copy in outs:
        copy.wait()


def local(a_tiles, a_where, a_count, b_slab):
    layers = lax.axis_size("layer")
    grid_size = lax.axis_size("col")
    row = lax.axis_index("row")
    col = lax.axis_index("col")
    layer = lax.axis_index("layer")
    slots, tile_size = a_tiles.shape[2], a_tiles.shape[-1]
    slab_cols = b_slab.shape[-1]
    rows = tile_size // layers

    slab_half = lax.dynamic_slice(b_slab[0, 0], (layer * tile_size, 0), (tile_size, slab_cols))
    slab = lax.all_gather(slab_half, ("row", "layer"), axis=0, tiled=True)

    live = jnp.arange(slots, dtype=jnp.int32) < a_count[0, 0]
    codes = jnp.where(live, a_where[0, 0], DEAD).astype(jnp.bfloat16)
    lines = []
    steps = (((0, 1), (1, 0)), ((1, 0), (0, 1)))
    for slot, (first, second) in enumerate(steps):
        piece = lax.dynamic_slice(a_tiles[0, 0], (slot, layer * rows, 0), (1, rows, tile_size))[0]
        code = jnp.broadcast_to(codes[slot], (PAD, tile_size))
        lines.append(gather_line(jnp.concatenate([piece, code], 0), first, layers))
    tiles = []
    for (first, second), line in zip(steps, lines):
        tiles += gather_line(jnp.concatenate(line, 0), second, layers)

    sign = 1 - 2 * layer
    offset = jnp.array([0, -1, 1, -2], jnp.int32) * sign
    here_x, here_y = col // SIDE, col % SIDE
    far_x, far_y = (here_x + offset) % SIDE, (here_y + offset) % SIDE
    source = jnp.stack([far_x[:, None] * SIDE + far_y[None, :], far_x[None, :] * SIDE + far_y[:, None]])
    slab_row = (row + source - col) % grid_size
    stride = rows + PAD
    found = jnp.concatenate([t.reshape(4, stride, tile_size)[:, rows, 0] for t in tiles])
    table = jnp.stack(
        [found.astype(jnp.int32), slab_row.reshape(-1), jnp.broadcast_to(layer, (32,))]
    )

    hbm = pl.BlockSpec(memory_space=pl.ANY)
    members = lax.axis_size("row") * layers
    flops = 2 * 32 * rows * tile_size * slab_cols
    keep, send, mass = pl.pallas_call(
        product_kernel,
        out_shape=(
            jax.ShapeDtypeStruct((rows, slab_cols), jnp.float32),
            pltpu.HBM((rows, slab_cols), jnp.float32),
            pltpu.HBM((members, 1, slab_cols), jnp.float32),
        ),
        in_specs=[pl.BlockSpec(memory_space=pltpu.SMEM)] + [hbm] * 9,
        out_specs=(hbm, hbm, hbm),
        scratch_shapes=[
            pltpu.VMEM((32, rows, tile_size), jnp.bfloat16),
            pltpu.VMEM((32, tile_size, slab_cols), jnp.bfloat16),
            pltpu.VMEM((SPAN + 1, rows, slab_cols), jnp.float32),
            pltpu.VMEM((members, 1, slab_cols), jnp.float32),
            pltpu.SMEM((20,), jnp.int32),
            pltpu.SMEM((20,), jnp.int32),
            pltpu.SMEM((20,), jnp.int32),
            pltpu.SemaphoreType.DMA((32,)),
            pltpu.SemaphoreType.DMA((32,)),
            pltpu.SemaphoreType.DMA((3,)),
        ],
        compiler_params=pltpu.CompilerParams(vmem_limit_bytes=44 << 20),
        cost_estimate=pl.CostEstimate(flops=flops, bytes_accessed=20 << 20, transcendentals=0),
    )(table, *tiles, slab)

    matrix_order = grid_size * SPAN * tile_size
    parts = lax.all_to_all(mass, ("row", "layer"), 0, 0, tiled=True)
    other = lax.ppermute(send, "layer", [(0, 1), (1, 0)])
    lower = layer == 0
    halves = jnp.where(lower, keep, other), jnp.where(lower, other, keep)
    column_mass = jnp.sum(parts, axis=(0, 1)) / matrix_order
    return jnp.concatenate(halves, 0) / (column_mass + 1e-06)


def solution(mesh):
    in_specs = (
        P("row", "col", None, None, None),
        P("row", "col", None),
        P("row", "col"),
        P("row", "col", None, None),
    )
    out_specs = P(("row", "layer"), "col")
    return jax.shard_map(local, mesh=mesh, in_specs=in_specs, out_specs=out_specs, check_vma=False)
```

```python
import functools

import jax
import jax.numpy as jnp
from jax import lax
from jax.experimental import pallas as pl
from jax.experimental.pallas import tpu as pltpu
from jax.sharding import PartitionSpec as P


SPAN = 2
SIDE = 4
PAD = 16
DEAD = SPAN * SPAN


def torus_pairs(step, layers):
    pairs = []
    for x in range(SIDE):
        for y in range(SIDE):
            for core in range(layers):
                sign = 1 - 2 * core
                to_x, to_y = (x + sign * step[0]) % SIDE, (y + sign * step[1]) % SIDE
                pairs.append(((x * SIDE + y) * layers + core, (to_x * SIDE + to_y) * layers + core))
    return pairs


def shift(value, step, sign, layers):
    return lax.ppermute(value, ("col", "layer"), torus_pairs((sign * step[0], sign * step[1]), layers))


def gather_line(value, step, layers):
    before = shift(value, step, 1, layers)
    after = shift(value, step, -1, layers)
    return [value, before, after, shift(before, step, 1, layers)]


def product_kernel(table, *refs):
    tile_refs = refs[:8]
    slab, keep, send, mass, pieces, blocks, sums, spread, order, target, source = refs[8:19]
    piece_sem, block_sem, out_sem = refs[19:]
    rows, depth = pieces.shape[1], blocks.shape[1]
    stride = rows + PAD

    def fetch_piece(item, tiles, inner):
        first = pl.multiple_of(inner * stride, PAD)
        return pltpu.make_async_copy(tiles.at[pl.ds(first, rows), :], pieces.at[item], piece_sem.at[item])

    def fetch_block(item):
        block = table[1, item] * SPAN + table[0, item] % SPAN
        first = pl.multiple_of(block * depth, depth)
        return pltpu.make_async_copy(slab.at[pl.ds(first, depth), :], blocks.at[item], block_sem.at[item])

    def add_product(item, block, half):
        sums[half] += jnp.dot(pieces[item], blocks[block], preferred_element_type=jnp.float32)

    for item in range(16):
        fetch_piece(item, tile_refs[item // 4], item % 4).start()
        fetch_block(item).start()
    sums[:SPAN] = jnp.zeros((SPAN,) + sums.shape[1:], jnp.float32)
    count = jnp.int32(0)
    for group in range(4):
        at_once = 1 if group == 0 else 4
        for first in range(group * 4, group * 4 + 4, at_once):
            for item in range(first, first + at_once):
                fetch_piece(item, tile_refs[0], 0).wait()
                fetch_block(item).wait()
            for item in range(first, first + at_once):
                add_product(item, item, table[0, item] // SPAN)
        for inner in range(4):
            item, mate = 16 + group * 4 + inner, inner * 4 + group
            live = table[0, item] < DEAD
            own = table[0, item] % SPAN != table[0, mate] % SPAN

            @pl.when(live)
            def _(item=item, inner=inner, group=group, count=count, own=own, mate=mate):
                fetch_piece(item, tile_refs[4 + group], inner).start()
                pl.when(own)(lambda: fetch_block(item).start())
                order[count] = item
                source[count] = jnp.where(own, item, mate)
                target[count] = table[0, item] // SPAN

            count = count + live.astype(jnp.int32)
    order[count] = 0
    source[count] = 0
    target[count] = SPAN
    batches = (count + 1) // 4

    def wait(place):
        item = order[place]
        fetch_piece(item, tile_refs[0], 0).wait()
        pl.when(source[place] == item)(lambda: fetch_block(item).wait())

    def batch(step, carry):
        for lane in range(4):
            place = step * 4 + lane
            pl.when(place < count)(functools.partial(wait, place))
        for lane in range(4):
            place = step * 4 + lane
            add_product(order[place], source[place], target[place])
        return carry

    def single(place, carry):
        wait(place)
        add_product(order[place], source[place], target[place])
        return carry

    lax.fori_loop(0, batches, batch, 0)
    lax.fori_loop(batches * 4, count, single, 0)
    mine = table[2, 0]
    outs = []
    total = jnp.zeros((1, sums.shape[2]), jnp.float32)
    for at, (half, out) in enumerate(((1 - mine, send), (mine, keep))):
        value = sums[half]
        value = value * value
        sums[half] = value
        outs.append(pltpu.make_async_copy(sums.at[half], out, out_sem.at[at]))
        outs[-1].start()
        total = total + jnp.sum(value, axis=0, keepdims=True)
    spread[...] = jnp.broadcast_to(total[None], spread.shape)
    outs.append(pltpu.make_async_copy(spread, mass, out_sem.at[2]))
    outs[-1].start()
    for copy in outs:
        copy.wait()


def finish_kernel(matrix_order, layer, parts, keep, other, out, halves, sems):
    rows = keep.shape[0]
    scale = jnp.sum(parts[...], axis=0) / matrix_order + 1e-06
    copies = []
    for at, (value, half) in enumerate(((keep, layer[0]), (other, 1 - layer[0]))):
        halves[at] = value[...] / scale
        first = pl.multiple_of(half * rows, rows)
        copies.append(pltpu.make_async_copy(halves.at[at], out.at[pl.ds(first, rows), :], sems.at[at]))
        copies[-1].start()
    for copy in copies:
        copy.wait()


def local(a_tiles, a_where, a_count, b_slab):
    layers = lax.axis_size("layer")
    grid_size = lax.axis_size("col")
    row = lax.axis_index("row")
    col = lax.axis_index("col")
    layer = lax.axis_index("layer")
    slots, tile_size = a_tiles.shape[2], a_tiles.shape[-1]
    slab_cols = b_slab.shape[-1]
    rows = tile_size // layers

    slab_half = lax.dynamic_slice(b_slab[0, 0], (layer * tile_size, 0), (tile_size, slab_cols))
    slab = lax.all_gather(slab_half, ("row", "layer"), axis=0, tiled=True)

    live = jnp.arange(slots, dtype=jnp.int32) < a_count[0, 0]
    codes = jnp.where(live, a_where[0, 0], DEAD).astype(jnp.bfloat16)
    lines = []
    steps = (((0, 1), (1, 0)), ((1, 0), (0, 1)))
    for slot, (first, second) in enumerate(steps):
        piece = lax.dynamic_slice(a_tiles[0, 0], (slot, layer * rows, 0), (1, rows, tile_size))[0]
        code = jnp.broadcast_to(codes[slot], (PAD, tile_size))
        lines.append(gather_line(jnp.concatenate([piece, code], 0), first, layers))
    tiles = []
    for (first, second), line in zip(steps, lines):
        tiles += gather_line(jnp.concatenate(line, 0), second, layers)

    sign = 1 - 2 * layer
    offset = jnp.array([0, -1, 1, -2], jnp.int32) * sign
    here_x, here_y = col // SIDE, col % SIDE
    far_x, far_y = (here_x + offset) % SIDE, (here_y + offset) % SIDE
    source = jnp.stack([far_x[:, None] * SIDE + far_y[None, :], far_x[None, :] * SIDE + far_y[:, None]])
    slab_row = (row + source - col) % grid_size
    stride = rows + PAD
    found = jnp.concatenate([t.reshape(4, stride, tile_size)[:, rows, 0] for t in tiles])
    table = jnp.stack(
        [found.astype(jnp.int32), slab_row.reshape(-1), jnp.broadcast_to(layer, (32,))]
    )

    hbm = pl.BlockSpec(memory_space=pl.ANY)
    members = lax.axis_size("row") * layers
    flops = 2 * 32 * rows * tile_size * slab_cols
    keep, send, mass = pl.pallas_call(
        product_kernel,
        out_shape=(
            jax.ShapeDtypeStruct((rows, slab_cols), jnp.float32),
            pltpu.HBM((rows, slab_cols), jnp.float32),
            pltpu.HBM((members, 1, slab_cols), jnp.float32),
        ),
        in_specs=[pl.BlockSpec(memory_space=pltpu.SMEM)] + [hbm] * 9,
        out_specs=(hbm, hbm, hbm),
        scratch_shapes=[
            pltpu.VMEM((32, rows, tile_size), jnp.bfloat16),
            pltpu.VMEM((32, tile_size, slab_cols), jnp.bfloat16),
            pltpu.VMEM((SPAN + 1, rows, slab_cols), jnp.float32),
            pltpu.VMEM((members, 1, slab_cols), jnp.float32),
            pltpu.SMEM((20,), jnp.int32),
            pltpu.SMEM((20,), jnp.int32),
            pltpu.SMEM((20,), jnp.int32),
            pltpu.SemaphoreType.DMA((32,)),
            pltpu.SemaphoreType.DMA((32,)),
            pltpu.SemaphoreType.DMA((3,)),
        ],
        compiler_params=pltpu.CompilerParams(vmem_limit_bytes=44 << 20),
        cost_estimate=pl.CostEstimate(flops=flops, bytes_accessed=20 << 20, transcendentals=0),
    )(table, *tiles, slab)

    matrix_order = grid_size * SPAN * tile_size
    parts = lax.all_to_all(mass, ("row", "layer"), 0, 0, tiled=True)
    other = lax.ppermute(send, "layer", [(0, 1), (1, 0)])
    return pl.pallas_call(
        functools.partial(finish_kernel, matrix_order),
        out_shape=jax.ShapeDtypeStruct((tile_size, slab_cols), jnp.float32),
        in_specs=[pl.BlockSpec(memory_space=pltpu.SMEM)] + [pl.BlockSpec(memory_space=pltpu.VMEM)] * 3,
        out_specs=pl.BlockSpec(memory_space=pl.ANY),
        scratch_shapes=[
            pltpu.VMEM((SPAN, rows, slab_cols), jnp.float32),
            pltpu.SemaphoreType.DMA((SPAN,)),
        ],
        compiler_params=pltpu.CompilerParams(vmem_limit_bytes=8 << 20),
    )(layer[None], parts, keep, other)


def solution(mesh):
    in_specs = (
        P("row", "col", None, None, None),
        P("row", "col", None),
        P("row", "col"),
        P("row", "col", None, None),
    )
    out_specs = P(("row", "layer"), "col")
    return jax.shard_map(local, mesh=mesh, in_specs=in_specs, out_specs=out_specs, check_vma=False)
```
